32 devices in a mesh: wide: 16 (over z, x, core), head: 2 (over y).
Axes of the slice: x: 2, y: 2, z: 4, core: 2. Of those that a mesh axis runs over, the one named last changes fastest.
Arguments:
- stream_in: bfloat16 [128, 16384], P(None, 'wide')
- queries: bfloat16 [128, 8192], P('wide', 'head')
- kv_cache: bfloat16 [128, 256, 8, 256], P('wide', None, 'head')
- lengths: int32 [128], P('wide'), may hold values from 2 to 256, as said below
- assign: int32 [128], replicated, may hold values from 0 to 127, as said below
- out_weight: bfloat16 [8192, 16384], P('head', 'wide'), may hold values from -0.0625 to 0.0625
- norm_gain: float32 [16384], P('wide'), may hold values from 0.1 to 1.9
- w_gate: bfloat16 [16384, 26624], P('wide', 'head'), may hold values from -0.046875 to 0.046875
- w_up: bfloat16 [16384, 26624], P('wide', 'head'), may hold values from -0.046875 to 0.046875
- down_weight: bfloat16 [26624, 16384], P('head', 'wide'), may hold values from -0.0390625 to 0.0390625
Outputs:
- result: bfloat16 [128, 16384], P(None, 'wide')
The draws below stay inside these ranges and needn't reach their ends.
Inputs may be any that keep to these rules, and one draw needn't show every extreme that they name: `assign`: each row of 0 to 127 is named by exactly one slot. `lengths`: some slot holds 256 live positions and some holds 2.
All inputs are finite; a program needn't handle non-finite values.
Results may differ from the reference program's by a relative error of at most 0.0056.
Values may be sent and summed in bfloat16 or wider, within the bound.
No kernel may reach another device: no remote copies, remote signals or barrier semaphores. Data moves between devices by JAX's collectives and lax.ppermute only.
A program may use at most 192 MiB of HBM per device.

```python
import math
import jax
import jax.numpy as jnp
from jax import lax

D = 16384
FF = 26624
KVH = 8
HD = 128
MAXLEN = 256
ROWS = 128
QD = 8192
G = 8


def slot_order(key):
    return jax.random.permutation(jax.random.fold_in(key, 7), ROWS).astype(jnp.int32)


def query_values(key):
    return jnp.clip(jax.random.normal(jax.random.fold_in(key, 13), (ROWS, QD), jnp.float32), -6.0, 6.0)


def draw_assign(key, part):
    return slot_order(key)


def draw_queries(key, part):
    return query_values(key).astype(jnp.bfloat16)


def draw_lengths(key, part):
    base = jax.random.randint(jax.random.fold_in(key, 17), (ROWS,), 2, MAXLEN + 1).astype(jnp.int32)
    picks = jax.random.permutation(jax.random.fold_in(key, 19), ROWS)
    base = base.at[picks[0]].set(MAXLEN)
    base = base.at[picks[1]].set(2)
    return base.astype(jnp.int32)


def draw_kv_cache(key, part):
    shape = (ROWS, MAXLEN, KVH, 2 * HD)
    values = jnp.clip(jax.random.normal(jax.random.fold_in(key, 23), shape, jnp.float32), -6.0, 6.0)
    return values.astype(jnp.bfloat16)


def draw_stream_in(key, part):
    columns = jnp.arange(D).astype(jnp.float32) / D
    base = jnp.clip(jax.random.normal(jax.random.fold_in(key, 29), (ROWS, D), jnp.float32), -6.0, 6.0)
    values = base * (0.6 + 1.2 * columns)[None, :]
    return values.astype(jnp.bfloat16)


def levels(stream_key, shape, shards, low, high):
    gain, own = 1.0, jax.random.fold_in(stream_key, 6)
    for axis_at, shards_of in shards:
        draws = jnp.exp(jax.random.uniform(jax.random.fold_in(own, axis_at), (shards_of,), jnp.float32, low / len(shards), high / len(shards)))
        gain = gain * jnp.repeat(draws, shape[axis_at] // shards_of).reshape([-1 if axis == axis_at else 1 for axis in range(len(shape))])
    return gain


def centred(key, extent, width, reach, split=(), dtype=jnp.bfloat16):
    drawn = jax.random.normal(key, extent, jnp.float32) * width
    if len(split) > 0:
        drawn = levels(key, extent, split, -0.22, 0.18) * drawn
    return jnp.clip(drawn, min=-reach, max=reach).astype(dtype)


def setup_inputs(seed: int = 0) -> dict:
    seeds = jax.random.split(jax.random.key(seed), 11)
    return {
        "stream_in": draw_stream_in(jax.random.fold_in(seeds[10], 71), 0),
        "queries": draw_queries(jax.random.fold_in(seeds[10], 71), 0),
        "kv_cache": draw_kv_cache(jax.random.fold_in(seeds[10], 71), 0),
        "lengths": draw_lengths(jax.random.fold_in(seeds[10], 71), 0),
        "assign": draw_assign(jax.random.fold_in(seeds[10], 71), 0),
        "out_weight": centred(seeds[5], (QD, D), QD ** -0.5, 0.0625, ((0, 2), (1, 16))),
        "norm_gain": jnp.clip(1.0 + 0.18 * jax.random.normal(seeds[6], (D,), jnp.float32), 0.1, 1.9),
        "w_gate": centred(seeds[7], (D, FF), D ** -0.5, 0.046875, ((0, 16), (1, 2))),
        "w_up": centred(seeds[8], (D, FF), D ** -0.5, 0.046875, ((0, 16), (1, 2))),
        "down_weight": centred(seeds[9], (FF, D), FF ** -0.5, 0.0390625, ((0, 2), (1, 16))),
    }


eps = 1e-05

def one_slot(packed):
    query_row, block, length = packed
    grouped = query_row.reshape(KVH, G, HD).astype(jnp.float32)
    key_part = block[:, :, :HD].astype(jnp.float32)
    value_part = block[:, :, HD:].astype(jnp.float32)
    scores = jnp.einsum('kgd,pkd->kgp', grouped, key_part) * (1.0 / math.sqrt(HD))
    live_mask = (jnp.arange(MAXLEN) < length)[None, None, :]
    scores = jnp.where(live_mask, scores, -1e+30)
    highest = lax.optimization_barrier(jnp.max(scores, axis=-1, keepdims=True))
    weights = jnp.where(live_mask, jnp.exp(scores - highest), 0.0)
    probs = (weights / lax.optimization_barrier(jnp.sum(weights, axis=-1, keepdims=True))).astype(jnp.bfloat16)
    context = jnp.einsum('kgp,pkd->kgd', probs.astype(jnp.float32), value_part)
    return context.reshape(QD).astype(jnp.bfloat16)

def reference(stream_in, queries, kv_cache, lengths, assign, out_weight, norm_gain, w_gate, w_up, down_weight):
    slot_queries = queries[assign]
    slot_context = lax.map(one_slot, (slot_queries, kv_cache, lengths))
    attn = jnp.zeros((ROWS, QD), jnp.bfloat16).at[assign].set(slot_context)
    projected = jnp.dot(attn, out_weight, preferred_element_type=jnp.float32)
    state = (stream_in.astype(jnp.float32) + projected).astype(jnp.bfloat16)
    state_f = state.astype(jnp.float32)
    squares = lax.optimization_barrier(jnp.sum(state_f * state_f, axis=1, keepdims=True)) / D
    normed = (state_f * lax.rsqrt(squares + eps) * norm_gain.astype(jnp.float32)).astype(jnp.bfloat16)
    gate = jnp.dot(normed, w_gate, preferred_element_type=jnp.float32)
    up_vals = jnp.dot(normed, w_up, preferred_element_type=jnp.float32)
    activated = (jax.nn.silu(gate) * up_vals).astype(jnp.bfloat16)
    down = jnp.dot(activated, down_weight, preferred_element_type=jnp.float32)
    return (state_f + down).astype(jnp.bfloat16)
```

```python
import math

import jax
import jax.numpy as jnp
import numpy as np
from jax import lax
from jax.experimental import pallas as pl
from jax.experimental.pallas import tpu as pltpu
from jax.sharding import PartitionSpec as P

D = 16384
eps = 1e-05
SHRINK = 2.0**-64
PARTS = 2
LANES = 128


def exchange_masks(count):
    bits = count.bit_length() - 1
    masks = [1 << bit for bit in range(1, bits)]
    if len(masks) > 1:
        masks[-1] |= masks[-2]
    return masks + [1]


def block_offsets(masks):
    offsets = []
    for block in range(1 << len(masks)):
        offset = 0
        for bit, mask in enumerate(masks):
            if block >> bit & 1:
                offset ^= mask
        offsets.append(offset)
    return np.array(offsets, np.int32)


def swap(value, axis, mask):
    return lax.ppermute(value, axis, [(i, i ^ mask) for i in range(lax.axis_size(axis))])


def gather_rows(value, masks):
    for mask in masks:
        value = jnp.concatenate([value, swap(value, "wide", mask)], axis=0)
    return value


def head_sum(value):
    step = 1
    while step < lax.axis_size("head"):
        sent = value.astype(jnp.bfloat16)
        value = sent.astype(jnp.float32) + swap(sent, "head", step).astype(jnp.float32)
        step *= 2
    return value


def slot_attention(own_queries, kv_cache, lengths):
    slot_count = kv_cache.shape[0]
    kv_local = kv_cache.shape[2]
    head_dim = kv_cache.shape[3] // 2
    grouped = own_queries.reshape(
        slot_count, kv_local, own_queries.shape[1] // (kv_local * head_dim), head_dim
    )
    key_part = kv_cache[:, :, :, :head_dim]
    value_part = kv_cache[:, :, :, head_dim:]
    scores = jnp.einsum(
        "skgd,spkd->skgp", grouped, key_part, preferred_element_type=jnp.float32
    ) * (1.0 / math.sqrt(head_dim))
    live_mask = (jnp.arange(kv_cache.shape[1])[None, :] < lengths[:, None])[:, None, None, :]
    scores = jnp.where(live_mask, scores, -1e30)
    highest = jnp.max(scores, axis=-1, keepdims=True)
    weights = jnp.where(live_mask, jnp.exp(scores - highest), 0.0)
    probs = (weights / jnp.sum(weights, axis=-1, keepdims=True)).astype(jnp.bfloat16)
    context = jnp.einsum("skgp,spkd->skgd", probs, value_part, preferred_element_type=jnp.float32)
    return context.reshape(slot_count, -1).astype(jnp.bfloat16)


def tile_of(extent, most=1024):
    units = extent // LANES
    return LANES * max(u for u in range(1, most // LANES + 1) if units % u == 0)


def gate_up_body(tiles, x_ref, extra_ref, gate_ref, up_ref, keep_ref, send_ref):
    half = x_ref.shape[0] // 2

    @pl.when(pl.program_id(0) < tiles)
    def _():
        for at, weight in enumerate((gate_ref, up_ref)):
            product = jnp.dot(x_ref[...], weight[...], preferred_element_type=jnp.float32)
            product = product.astype(jnp.bfloat16)
            keep_ref[at] = product[:half]
            send_ref[at] = product[half:]

    @pl.when(pl.program_id(0) == tiles)
    def _():
        for at in range(2):
            keep_ref[at, :, :LANES] = extra_ref[:half]
            send_ref[at, :, :LANES] = extra_ref[half:]


def gate_up(x, extra, w_gate, w_up, first, tiles, tile, with_extra):
    rows, depth = x.shape
    half = rows // 2
    columns = tiles * tile + (LANES if with_extra else 0)
    out = jax.ShapeDtypeStruct((2, half, columns), jnp.bfloat16)
    weight = pl.BlockSpec((depth, tile), lambda j: (0, first + jnp.minimum(j, tiles - 1)))
    block = pl.BlockSpec((2, half, tile), lambda j: (0, 0, j))
    return pl.pallas_call(
        lambda *refs: gate_up_body(tiles, *refs),
        grid=(tiles + (1 if with_extra else 0),),
        in_specs=[
            pl.BlockSpec((rows, depth), lambda j: (0, 0)),
            pl.BlockSpec((rows, LANES), lambda j: (0, 0)),
            weight,
            weight,
        ],
        out_specs=[block, block],
        out_shape=[out, out],
        cost_estimate=pl.CostEstimate(
            flops=4 * rows * depth * tiles * tile,
            bytes_accessed=4 * depth * tiles * tile + 4 * rows * tiles * tile,
            transcendentals=0,
        ),
        name="gate_up",
    )(x, extra, w_gate, w_up)


def down_body(act_ref, weight_ref, before_ref, total_ref):
    product = jnp.dot(act_ref[...], weight_ref[...], preferred_element_type=jnp.float32)

    @pl.when(pl.program_id(0) == 0)
    def _():
        total_ref[...] = before_ref[...] + product

    @pl.when(pl.program_id(0) > 0)
    def _():
        total_ref[...] += product


def down(act, down_weight, before, first, tiles, tile):
    rows = act.shape[0]
    columns = down_weight.shape[1]
    whole = pl.BlockSpec((rows, columns), lambda j: (0, 0))
    return pl.pallas_call(
        down_body,
        grid=(tiles,),
        in_specs=[
            pl.BlockSpec((rows, tile), lambda j: (0, j)),
            pl.BlockSpec((tile, columns), lambda j: (first + j, 0)),
            whole,
        ],
        out_specs=whole,
        out_shape=jax.ShapeDtypeStruct((rows, columns), jnp.float32),
        cost_estimate=pl.CostEstimate(
            flops=2 * rows * columns * tiles * tile,
            bytes_accessed=2 * columns * tiles * tile + 2 * rows * tiles * tile,
            transcendentals=0,
        ),
        name="down",
    )(act, down_weight, before)


def scatter_sums(keep, send, masks, order):
    core_bit = len(masks) - 1
    value = keep.astype(jnp.float32) + swap(send, "wide", masks[core_bit]).astype(jnp.float32)
    left = list(range(core_bit - 1, -1, -1))
    for bit in order:
        at = left.index(bit)
        left.remove(bit)
        pair, rows, columns = value.shape
        split = value.astype(jnp.bfloat16).reshape(pair, 1 << at, 2, rows >> (at + 1), columns)
        kept = split[:, :, 0].reshape(pair, rows // 2, columns)
        sent = split[:, :, 1].reshape(pair, rows // 2, columns)
        value = kept.astype(jnp.float32) + swap(sent, "wide", masks[bit]).astype(jnp.float32)
    return value


def gather_act(act, masks, order):
    rows, columns = act.shape
    steps = list(order) + [len(masks) - 1]
    for bit in steps:
        act = jnp.concatenate([act, swap(act, "wide", masks[bit])], axis=0)
    count = len(steps)
    if steps != list(range(count)):
        act = act.reshape((2,) * count + (rows, columns))
        where = [count - 1 - steps.index(bit) for bit in range(count - 1, -1, -1)]
        act = act.transpose(where + [count, count + 1]).reshape(rows << count, columns)
    return act


def local(
    stream_in, queries, kv_cache, lengths, assign, out_weight, norm_gain, w_gate, w_up, down_weight
):
    wide = lax.axis_size("wide")
    me = lax.axis_index("wide")
    slot_count = kv_cache.shape[0]
    rows = stream_in.shape[0]
    masks = exchange_masks(wide)
    offsets = jnp.repeat(jnp.asarray(block_offsets(masks)), slot_count)
    place = (offsets ^ me) * slot_count + jnp.arange(rows, dtype=jnp.int32) % slot_count
    named = jnp.take(assign, place)

    gathered = gather_rows(queries, masks)
    own_rows = lax.dynamic_slice_in_dim(assign, me * slot_count, slot_count, 0)
    pick = (own_rows[:, None] == place[None, :]).astype(jnp.bfloat16)
    own_queries = jnp.dot(pick, gathered, preferred_element_type=jnp.float32).astype(jnp.bfloat16)
    context = gather_rows(slot_attention(own_queries, kv_cache, lengths), masks)
    projected = head_sum(jnp.dot(context, out_weight, preferred_element_type=jnp.float32))
    stream = jnp.take(stream_in, named, axis=0)
    state = (stream.astype(jnp.float32) + projected).astype(jnp.bfloat16)
    state_f = state.astype(jnp.float32)
    x = (state_f * (norm_gain * SHRINK)).astype(jnp.bfloat16)
    squares = jnp.sum(state_f * state_f, axis=1, keepdims=True)
    high = squares.astype(jnp.bfloat16)
    low = (squares - high.astype(jnp.float32)).astype(jnp.bfloat16)
    lane = jnp.arange(LANES)[None, :]
    zero = jnp.zeros((), jnp.bfloat16)
    extra = jnp.where(lane == me, high, jnp.where(lane == me + wide, low, zero))

    feed_local = w_gate.shape[1]
    tile = tile_of(feed_local)
    tiles = feed_local // tile
    bounds = [tiles * part // PARTS for part in range(PARTS + 1)]
    dims = list(range(len(masks) - 1))
    orders = [dims[::-1], dims]
    sums = []
    for part in range(PARTS):
        keep, send = gate_up(
            x, extra, w_gate, w_up, bounds[part], bounds[part + 1] - bounds[part], tile, part == 0
        )
        sums.append(scatter_sums(keep, send, masks, orders[part % 2]))
    width = (bounds[1] - bounds[0]) * tile
    own_squares = jnp.sum(sums[0][0, :, width:], axis=1, keepdims=True)
    scale = lax.rsqrt(own_squares / D + eps) * (1.0 / SHRINK)
    total = jnp.zeros((rows, down_weight.shape[1]), jnp.float32)
    for part in range(PARTS):
        width = (bounds[part + 1] - bounds[part]) * tile
        gate = sums[part][0, :, :width] * scale
        up = sums[part][1, :, :width] * scale
        act = (jax.nn.silu(gate) * up).astype(jnp.bfloat16)
        act = gather_act(act, masks, orders[part % 2][::-1])
        total = down(act, down_weight, total, bounds[part], bounds[part + 1] - bounds[part], tile)
    result = (state_f + head_sum(total)).astype(jnp.bfloat16)
    ordered = jnp.sum(
        jnp.where(named[None, :] == jnp.arange(rows)[:, None], jnp.arange(rows)[None, :], 0), axis=1
    )
    return jnp.take(result, ordered, axis=0)


def solution(mesh):
    placed = (
        P(None, "wide"),
        P("wide", "head"),
        P("wide", None, "head", None),
        P("wide"),
        P(),
        P("head", "wide"),
        P("wide"),
        P("wide", "head"),
        P("wide", "head"),
        P("head", "wide"),
    )
    return jax.shard_map(
        local, mesh=mesh, in_specs=placed, out_specs=P(None, "wide"), check_vma=False
    )
```
